256 devices in a mesh: dp: 16 (over x_lo, y, core), ctx: 16 (over z, x_hi).
Axes of the slice: x: 4 (x_hi: 2, x_lo: 2; x = x_hi * 2 + x_lo), y: 4, z: 8, core: 2. Of those that a mesh axis runs over, the one named last changes fastest.
Arguments:
- input_gate: bfloat16 [512, 131072], P('dp', 'ctx'), may hold values from -6 to 6
- output_gate: bfloat16 [512, 131072], P('dp', 'ctx'), may hold values from -6 to 6
- values: bfloat16 [512, 131072], P('dp', 'ctx'), may hold values from -6 to 6
- cotangent: bfloat16 [512, 131072], P('dp', 'ctx'), may hold values from -6 to 6
- filter_raw: bfloat16 [16, 131072], P(None, 'ctx'), may hold values from -6 to 6
- filter_decay: float32 [16], replicated, may hold values from 0.25 to 2
- skip_gain: float32 [512], P('dp'), may hold values from -4 to 4
Outputs:
- outputs: bfloat16 [512, 131072], P('dp', 'ctx')
- grad_input_gate: bfloat16 [512, 131072], P('dp', 'ctx')
- grad_output_gate: bfloat16 [512, 131072], P('dp', 'ctx')
- grad_values: bfloat16 [512, 131072], P('dp', 'ctx')
- grad_filter: float32 [16, 131072], P(None, 'ctx')
The draws below stay inside these ranges and needn't reach their ends.
All inputs are finite; a program needn't handle non-finite values.
Results may differ from the reference program's by a relative error of at most 0.018.
Values may be sent and summed in bfloat16 or wider, within the bound.
A program may use at most 64 MiB of HBM per device.

```python
import math
import jax
import jax.numpy as jnp
from jax import lax

N1 = 512
N2 = 512
CHANNELS = 512
FILTERS = 16
FFT_LEN = 262144
SEQ = 131072


def shard_levels(rng, extent, shards, least, high):
    loudness, own = 1.0, jax.random.fold_in(rng, 6)
    for dim, parts in shards:
        heights = jnp.exp(jax.random.uniform(jax.random.fold_in(own, dim), (parts,), jnp.float32, least / len(shards), high / len(shards)))
        loudness = loudness * jnp.repeat(heights, extent[dim] // parts).reshape([-1 if axis == dim else 1 for axis in range(len(extent))])
    return loudness


def scatter_about(rng, shape, deviation, limit, cuts=(), kind=jnp.bfloat16):
    values = deviation * jax.random.normal(rng, shape, jnp.float32)
    if cuts:
        values = values * shard_levels(rng, shape, cuts, -0.22, 0.18)
    return jnp.clip(values, -limit, limit).astype(kind)


def setup_inputs(seed: int = 0) -> dict:
    arg_keys = jax.random.split(jax.random.key(seed), 8)
    input_gate = scatter_about(arg_keys[0], (CHANNELS, SEQ), 1.0, 6.0, ((0, 16), (1, 16)))
    output_gate = scatter_about(arg_keys[1], (CHANNELS, SEQ), 1.0, 6.0, ((0, 16), (1, 16)))
    values = scatter_about(arg_keys[2], (CHANNELS, SEQ), 1.0, 6.0, ((0, 16), (1, 16)))
    cotangent = scatter_about(arg_keys[3], (CHANNELS, SEQ), 1.0, 6.0, ((0, 16), (1, 16)))
    filter_raw = scatter_about(arg_keys[4], (FILTERS, SEQ), 1.0, 6.0, ((1, 16),))
    filter_decay = jnp.clip(jnp.exp(jax.random.uniform(arg_keys[5], (FILTERS,), jnp.float32, math.log(0.25), math.log(2.0))), 0.25, 2.0)
    skip_gain = scatter_about(arg_keys[6], (CHANNELS,), 1.0, 4.0, ((0, 16),), jnp.float32)
    return {"input_gate": input_gate, "output_gate": output_gate, "values": values, "cotangent": cotangent, "filter_raw": filter_raw, "filter_decay": filter_decay, "skip_gain": skip_gain}


two_pi = 2.0 * math.pi


def product(form, left, right):
    return jnp.einsum(form, left.astype(jnp.float32), right.astype(jnp.float32), precision=lax.Precision.HIGHEST)


def dft_tables(row_total):
    first_index = jnp.arange(N1, dtype=jnp.int32)
    source_rows = jnp.arange(row_total, dtype=jnp.int32)
    first_angles = ((first_index[:, None] * source_rows[None, :]) % N1).astype(jnp.float32) * (two_pi / N1)
    second_index = jnp.arange(N2, dtype=jnp.int32)
    second_angles = ((second_index[:, None] * second_index[None, :]) % N2).astype(jnp.float32) * (two_pi / N2)
    return (jnp.cos(first_angles).astype(jnp.bfloat16), (-jnp.sin(first_angles)).astype(jnp.bfloat16),
            jnp.cos(second_angles).astype(jnp.bfloat16), (-jnp.sin(second_angles)).astype(jnp.bfloat16))


def twiddle_table(spectrum_rows, columns):
    angles = ((spectrum_rows[:, None] * columns[None, :]) % FFT_LEN).astype(jnp.float32) * (two_pi / FFT_LEN)
    return jnp.cos(angles), -jnp.sin(angles)


def forward_signal(signal, tables, turn):
    first_real, first_imaginary, second_real, second_imaginary = tables
    turn_real, turn_imaginary = turn
    product_real = product("km,bmn->bkn", first_real, signal)
    product_imaginary = product("km,bmn->bkn", first_imaginary, signal)
    turned_real = (product_real * turn_real - product_imaginary * turn_imaginary).astype(jnp.bfloat16)
    turned_imaginary = (product_real * turn_imaginary + product_imaginary * turn_real).astype(jnp.bfloat16)
    spectrum_real = (product("bkn,nl->bkl", turned_real, second_real)
                     - product("bkn,nl->bkl", turned_imaginary, second_imaginary))
    spectrum_imaginary = (product("bkn,nl->bkl", turned_real, second_imaginary)
                          + product("bkn,nl->bkl", turned_imaginary, second_real))
    return spectrum_real, spectrum_imaginary


def inverse_signal(spectrum_real, spectrum_imaginary, tables, turn):
    first_real, first_imaginary, second_real, second_imaginary = tables
    turn_real, turn_imaginary = turn
    back_real = (product("bkn,nl->bkl", spectrum_real, second_real)
                 + product("bkn,nl->bkl", spectrum_imaginary, second_imaginary))
    back_imaginary = (product("bkn,nl->bkl", spectrum_imaginary, second_real)
                      - product("bkn,nl->bkl", spectrum_real, second_imaginary))
    inverse_scale = 1.0 / FFT_LEN
    rotated_real = ((back_real * turn_real + back_imaginary * turn_imaginary) * inverse_scale).astype(jnp.bfloat16)
    rotated_imaginary = ((back_imaginary * turn_real - back_real * turn_imaginary) * inverse_scale).astype(jnp.bfloat16)
    result = (product("km,bkn->bmn", first_real, rotated_real)
              + product("km,bkn->bmn", first_imaginary, rotated_imaginary))
    return result.astype(jnp.bfloat16)


def reference(input_gate, output_gate, values, cotangent, filter_raw, filter_decay, skip_gain):
    row_total = SEQ // N2
    tables = dft_tables(row_total)
    turn = twiddle_table(jnp.arange(N1, dtype=jnp.int32), jnp.arange(N2, dtype=jnp.int32))
    all_positions = jnp.arange(SEQ, dtype=jnp.int32).astype(jnp.float32)
    envelope = jnp.exp(-filter_decay[:, None] * (all_positions[None, :] / SEQ))
    filter_scale = SEQ ** -0.5
    filter_taps = (filter_raw.astype(jnp.float32) * envelope * filter_scale).astype(jnp.bfloat16)
    spec_real, spec_imaginary = forward_signal(filter_taps.reshape(FILTERS, row_total, N2), tables, turn)
    filter_real = spec_real.astype(jnp.bfloat16).astype(jnp.float32)
    filter_imaginary = spec_imaginary.astype(jnp.bfloat16).astype(jnp.float32)
    groups = CHANNELS // FILTERS

    def grouped(array):
        return array.reshape(groups, FILTERS, SEQ)

    def one_group(operands):
        gate_input, gate_output, value_rows, cotangent_rows, skip_rows = operands
        mixed_input = (gate_input.astype(jnp.float32) * value_rows.astype(jnp.float32)).astype(jnp.bfloat16)
        weighted = (cotangent_rows.astype(jnp.float32) * gate_output.astype(jnp.float32)).astype(jnp.bfloat16)
        mix_real, mix_imaginary = forward_signal(mixed_input.reshape(FILTERS, row_total, N2), tables, turn)
        weight_real, weight_imaginary = forward_signal(weighted.reshape(FILTERS, row_total, N2), tables, turn)
        convolved = inverse_signal((mix_real * filter_real - mix_imaginary * filter_imaginary).astype(jnp.bfloat16),
                                   (mix_real * filter_imaginary + mix_imaginary * filter_real).astype(jnp.bfloat16),
                                   tables, turn).reshape(FILTERS, SEQ)
        correlated = inverse_signal((filter_real * weight_real + filter_imaginary * weight_imaginary).astype(jnp.bfloat16),
                                    (filter_real * weight_imaginary - filter_imaginary * weight_real).astype(jnp.bfloat16),
                                    tables, turn).reshape(FILTERS, SEQ)
        lagged = inverse_signal((mix_real * weight_real + mix_imaginary * weight_imaginary).astype(jnp.bfloat16),
                                (mix_real * weight_imaginary - mix_imaginary * weight_real).astype(jnp.bfloat16),
                                tables, turn).reshape(FILTERS, SEQ)
        summed = convolved.astype(jnp.float32) + skip_rows[:, None] * mixed_input.astype(jnp.float32)
        outputs = (gate_output.astype(jnp.float32) * summed).astype(jnp.bfloat16)
        grad_two = (cotangent_rows.astype(jnp.float32) * summed).astype(jnp.bfloat16)
        back_total = correlated.astype(jnp.float32) + skip_rows[:, None] * weighted.astype(jnp.float32)
        grad_one = (back_total * value_rows.astype(jnp.float32)).astype(jnp.bfloat16)
        grad_three = (back_total * gate_input.astype(jnp.float32)).astype(jnp.bfloat16)
        return outputs, grad_one, grad_two, grad_three, lagged

    results = lax.map(one_group, (grouped(input_gate), grouped(output_gate), grouped(values),
                                  grouped(cotangent), skip_gain.reshape(groups, FILTERS)))
    lag_total = jnp.sum(results[4].astype(jnp.float32), axis=0)
    grad_filter = lag_total * envelope * filter_scale
    return (results[0].reshape(CHANNELS, SEQ), results[1].reshape(CHANNELS, SEQ),
            results[2].reshape(CHANNELS, SEQ), results[3].reshape(CHANNELS, SEQ), grad_filter)
```

```python
import functools

import jax
import jax.numpy as jnp
import numpy as np
from jax import lax
from jax.experimental import pallas as pl
from jax.experimental.pallas import tpu as pltpu
from jax.sharding import PartitionSpec as P

N = 512
FFT_LEN = N * N
SEQ = FFT_LEN // 2
CTX = 16
ROWS = 16
LOCAL = ROWS * N
HALF = N // 2
QUARTER = N // 4
SCALE = SEQ**-0.5
CHUNK = 256
MESH = pl.DeviceIdType.MESH
F32 = jnp.float32
BF16 = jnp.bfloat16


def constant_tables():
    index = np.arange(N)
    angle = (index[:, None] * index[None, :] % N) * (2.0 * np.pi / N)
    roots = np.stack([np.cos(angle), np.sin(angle)]).astype(jnp.bfloat16)
    coarse = np.arange(N // ROWS)[:, None] * ROWS * index[None, :] * (2.0 * np.pi / FFT_LEN)
    fine = np.arange(ROWS)[:, None] * index[None, :] * (2.0 * np.pi / FFT_LEN)
    both = np.concatenate([coarse, fine], axis=0)
    turns = np.stack([np.cos(both), -np.sin(both)]).astype(np.float32)
    return roots, turns


def dot(left, right):
    return jnp.dot(left, right, preferred_element_type=F32)


def times(ar, ai, br, bi):
    return ar * br - ai * bi, ar * bi + ai * br


def conj_times(ar, ai, br, bi):
    return ar * br + ai * bi, ar * bi - ai * br


def joined(real, imaginary):
    return jnp.concatenate([real, imaginary], axis=1).astype(BF16)


def parts(value):
    return value[:, :N], value[:, N:]


def step_of(i):
    j = i // 2
    return 4 + (1 - 2 * (j % 2)) * ((j + 1) // 2), 1 - i % 2


def kernel(
    ig_hbm, va_hbm, ct_hbm, og_hbm, fr_hbm, decay_hbm, skip_hbm, roots_hbm, turns_hbm,
    out_hbm, gig_hbm, gog_hbm, gva_hbm, gf_hbm,
    ig, va, ct, og, fr, decay, skip, roots, turns,
    out, gig, gog, gva, gf,
    first, first_back, second, second_back, wr, wi, perm,
    mixed, weighted, send_m, recv_m, send_w, recv_w,
    send_t, taps_q, taps, spec_h, spec_m, turned, turned_lag,
    send_c, recv_c, send_u, recv_u, summed,
    lag_q, lag_y, lag_z, lag_f, lag_x, lag_g, lag,
    in_sem, out_sem, ctx_send, ctx_recv, dp_send, dp_recv,
):
    dp = lax.axis_index("dp")
    me = lax.axis_index("ctx")
    my_z, my_x = me // 2, me % 2
    low, my_y, core = dp // 8, (dp // 2) % 4, dp % 2

    def ctx_peer(i):
        dz, dx = step_of(i)
        return ((my_z + dz) % 8) * 2 + (my_x + dx) % 2

    def y_peer(j):
        y = (my_y + 1 + j) % 4
        return y, low * 8 + y * 2 + core

    def side_peer(j):
        flip = j + 1
        other_low = (low + flip // 2) % 2
        other_core = (core + flip % 2) % 2
        return other_low * 8 + my_y * 2 + other_core

    barrier = pltpu.get_barrier_semaphore()

    def greet(i, carry):
        pl.semaphore_signal(barrier, inc=1, device_id={"ctx": ctx_peer(i)}, device_id_type=MESH)
        return carry

    lax.fori_loop(0, CTX - 1, greet, 0)
    for j in range(3):
        pl.semaphore_signal(barrier, inc=1, device_id={"dp": y_peer(j)[1]}, device_id_type=MESH)
        pl.semaphore_signal(barrier, inc=1, device_id={"dp": side_peer(j)}, device_id_type=MESH)

    loads = [
        pltpu.make_async_copy(source, target, in_sem.at[i])
        for i, (source, target) in enumerate(
            [
                (decay_hbm, decay), (fr_hbm, fr), (ig_hbm, ig), (va_hbm, va), (ct_hbm, ct),
                (og_hbm, og), (roots_hbm, roots), (turns_hbm, turns), (skip_hbm, skip),
            ]
        )
    ]
    for load in loads:
        load.start()

    row = lax.broadcasted_iota(jnp.int32, (256, 256), 0)
    col = lax.broadcasted_iota(jnp.int32, (256, 256), 1)
    perm[...] = jnp.where(col == (row % 16) * 16 + row // 16, 1.0, 0.0).astype(BF16)

    def column(line, count):
        r = lax.broadcasted_iota(jnp.int32, (count, count), 0)
        c = lax.broadcasted_iota(jnp.int32, (count, count), 1)
        return jnp.sum(jnp.where(r == c, line, 0.0), axis=1, keepdims=True)

    loads[0].wait()
    loads[1].wait()
    decay_column = column(decay[...], 16)

    def envelope(start, width):
        place = start + lax.broadcasted_iota(jnp.int32, (16, width), 1)
        place = (me * LOCAL + place).astype(F32)
        return jnp.exp(-decay_column * (place * (1.0 / SEQ)))

    def taps_row(r, carry):
        start = pl.multiple_of(r * N + my_y * QUARTER, QUARTER)
        raw = fr[:, pl.ds(start, QUARTER)].astype(F32)
        made = (raw * envelope(start, QUARTER) * SCALE).astype(BF16)
        turned[pl.ds(pl.multiple_of(r * 16, 16), 16), 0:QUARTER] = made
        return carry

    lax.fori_loop(0, ROWS, taps_row, 0)
    send_t[...] = dot(perm[...], turned[0:256, 0:QUARTER]).astype(BF16)

    def multiply(left, right, target, send):
        for g in range(2):

            def block(r, carry, g=g):
                lanes = pl.ds(pl.multiple_of(r * N, N), N)
                a = left[g * 16 : g * 16 + 16, lanes].astype(F32)
                b = right[g * 16 : g * 16 + 16, lanes].astype(F32)
                target[g, pl.ds(pl.multiple_of(r * 16, 16), 16), :] = (a * b).astype(BF16)
                return carry

            lax.fori_loop(0, ROWS, block, 0)
            send[g] = dot(perm[...], target[g]).astype(BF16).reshape(16, 16, N)

    def exchange(k, send, recv):
        def copy(i):
            return pltpu.make_async_remote_copy(
                src_ref=send.at[:, ctx_peer(i)],
                dst_ref=recv.at[:, me],
                send_sem=ctx_send.at[k, i],
                recv_sem=ctx_recv.at[k, i],
                device_id={"ctx": ctx_peer(i)},
                device_id_type=MESH,
            )

        return copy

    def small_exchange(k, send, recv):
        def copy(i):
            return pltpu.make_async_remote_copy(
                src_ref=send.at[pl.ds(pl.multiple_of(ctx_peer(i) * 16, 16), 16), :],
                dst_ref=recv.at[pl.ds(pl.multiple_of(me * 16, 16), 16), :],
                send_sem=ctx_send.at[k, i],
                recv_sem=ctx_recv.at[k, i],
                device_id={"ctx": ctx_peer(i)},
                device_id_type=MESH,
            )

        return copy

    def over(copy, action, count=CTX - 1):
        def one(i, carry):
            getattr(copy(i), action)()
            return carry

        lax.fori_loop(0, count, one, 0)

    def keep(send, recv):
        recv[:, pl.ds(me, 1)] = send[:, pl.ds(me, 1)]

    def keep_small(send, recv):
        rows = pl.ds(pl.multiple_of(me * 16, 16), 16)
        recv[rows, :] = send[rows, :]

    loads[2].wait()
    loads[3].wait()
    pl.semaphore_wait(barrier, CTX - 1 + 6)
    copy_t = small_exchange(0, send_t, taps_q.at[my_y])
    over(copy_t, "start")
    multiply(ig, va, mixed, send_m)
    copy_m = exchange(1, send_m, recv_m)
    over(copy_m, "start")
    loads[4].wait()
    loads[5].wait()
    multiply(ct, og, weighted, send_w)
    copy_w = exchange(2, send_w, recv_w)
    over(copy_w, "start")
    keep_small(send_t, taps_q.at[my_y])
    keep(send_m, recv_m)
    keep(send_w, recv_w)

    loads[6].wait()
    loads[7].wait()
    loads[8].wait()
    cosine, sine = roots[0], roots[1]
    first[0:N, 0:HALF] = cosine[:, 0:HALF]
    first[0:N, HALF:N] = sine[:, 0:HALF]
    first[N:, 0:HALF] = -sine[:, 0:HALF]
    first[N:, HALF:N] = cosine[:, 0:HALF]
    first_back[0:HALF, 0:N] = cosine[0:HALF]
    first_back[0:HALF, N:] = -sine[0:HALF]
    first_back[HALF:, 0:N] = sine[0:HALF]
    first_back[HALF:, N:] = cosine[0:HALF]
    second[0:N, 0:N] = cosine
    second[0:N, N:] = -sine
    second[N:, 0:N] = sine
    second[N:, N:] = cosine
    second_back[0:N, 0:N] = cosine
    second_back[0:N, N:] = sine
    second_back[N:, 0:N] = -sine
    second_back[N:, N:] = cosine
    fine_r, fine_i = turns[0, 32:48, :], turns[1, 32:48, :]

    def turn_rows(a, carry):
        rows = pl.ds(pl.multiple_of(a * 16, 16), 16)
        tr, ti = times(turns[0, pl.ds(a, 1), :], turns[1, pl.ds(a, 1), :], fine_r, fine_i)
        wr[rows, :] = tr
        wi[rows, :] = ti
        return carry

    lax.fori_loop(0, N // 16, turn_rows, 0)

    over(copy_t, "wait_recv")

    def share_t(j):
        return pltpu.make_async_remote_copy(
            src_ref=taps_q.at[my_y],
            dst_ref=taps_q.at[my_y],
            send_sem=dp_send.at[0, j],
            recv_sem=dp_recv.at[0, j],
            device_id={"dp": y_peer(j)[1]},
            device_id_type=MESH,
        )

    over(share_t, "start", 3)
    over(share_t, "wait_recv", 3)
    for q in range(4):
        taps[:, q * QUARTER : (q + 1) * QUARTER] = taps_q[q]

    def forward(start, width, block):
        rows = pl.ds(start, CHUNK)
        pr = dot(first[rows, 0:width], block)
        pi = dot(first[pl.ds(start + N, CHUNK), 0:width], block)
        return dot(joined(*times(pr, pi, wr[rows, :], wi[rows, :])), second[...])

    def backward(start, spectrum, target):
        rows = pl.ds(start, CHUNK)
        br, bi = parts(dot(spectrum, second_back[...]))
        sr, si = conj_times(wr[rows, :], wi[rows, :], br, bi)
        target[rows, :] = (sr * (1.0 / FFT_LEN)).astype(BF16)
        target[pl.ds(start + N, CHUNK), :] = (si * (1.0 / FFT_LEN)).astype(BF16)

    def chunks(body):
        def one(i, carry):
            body(pl.multiple_of(i * CHUNK, CHUNK))
            return carry

        lax.fori_loop(0, N // CHUNK, one, 0)

    def filter_chunk(start):
        spec_h[pl.ds(start, CHUNK), :] = forward(start, HALF, taps[...]).astype(BF16)

    chunks(filter_chunk)

    over(copy_m, "wait_recv")

    def mix_chunk(start):
        rows = pl.ds(start, CHUNK)
        spectrum = forward(start, N, recv_m[...].reshape(N, N))
        spec_m[rows, :] = spectrum
        hr, hi = parts(spec_h[rows, :].astype(F32))
        backward(start, joined(*times(*parts(spectrum), hr, hi)), turned)

    chunks(mix_chunk)
    for g in range(2):
        made = dot(first_back[g * HALF : (g + 1) * HALF, :], turned[...])
        send_c[g] = made.astype(BF16).reshape(16, 16, N)
    copy_c = exchange(3, send_c, recv_c)
    over(copy_c, "start")
    keep(send_c, recv_c)

    over(copy_w, "wait_recv")

    def weight_chunk(start):
        rows = pl.ds(start, CHUNK)
        spectrum = parts(forward(start, N, recv_w[...].reshape(N, N)))
        hr, hi = parts(spec_h[rows, :].astype(F32))
        backward(start, joined(*conj_times(hr, hi, *spectrum)), turned)
        mr, mi = parts(spec_m[rows, :])
        backward(start, joined(*conj_times(mr, mi, *spectrum)), turned_lag)

    chunks(weight_chunk)
    lagged = dot(first_back[0:HALF, :], turned_lag[...]).astype(BF16)
    for q in range(4):
        lag_q[q] = lagged[:, q * QUARTER : (q + 1) * QUARTER]

    def scatter_y(j):
        y, device = y_peer(j)
        return pltpu.make_async_remote_copy(
            src_ref=lag_q.at[y],
            dst_ref=lag_y.at[my_y],
            send_sem=dp_send.at[1, j],
            recv_sem=dp_recv.at[1, j],
            device_id={"dp": device},
            device_id_type=MESH,
        )

    over(scatter_y, "start", 3)
    lag_y[pl.ds(my_y, 1)] = lag_q[pl.ds(my_y, 1)]
    for g in range(2):
        made = dot(first_back[g * HALF : (g + 1) * HALF, :], turned[...])
        send_u[g] = made.astype(BF16).reshape(16, 16, N)
    over(scatter_y, "wait_recv", 3)
    lag_z[...] = sum(lag_y[y].astype(F32) for y in range(4)).astype(BF16)
    copy_z = small_exchange(4, lag_z, lag_f)
    over(copy_z, "start")
    copy_u = exchange(5, send_u, recv_u)
    over(copy_u, "start")
    keep_small(lag_z, lag_f)
    keep(send_u, recv_u)

    skip_column = column(skip[...], 32)

    def finish(recv, base, left, right, first_out, second_out):
        for g in range(2):
            gain = skip_column[g * 16 : g * 16 + 16]
            summed[...] = dot(perm[...], recv[g].reshape(256, N))

            def block(r, carry, g=g, gain=gain):
                rows = pl.ds(pl.multiple_of(r * 16, 16), 16)
                lanes = pl.ds(pl.multiple_of(r * N, N), N)
                total = summed[rows, :] + gain * base[g, rows, :].astype(F32)
                place = slice(g * 16, g * 16 + 16)
                first_out[place, lanes] = (left[place, lanes].astype(F32) * total).astype(BF16)
                second_out[place, lanes] = (right[place, lanes].astype(F32) * total).astype(BF16)
                return carry

            lax.fori_loop(0, ROWS, block, 0)

    over(copy_z, "wait_recv")

    def share_side(j):
        return pltpu.make_async_remote_copy(
            src_ref=lag_f,
            dst_ref=lag_x.at[j],
            send_sem=dp_send.at[2, j],
            recv_sem=dp_recv.at[2, j],
            device_id={"dp": side_peer(j)},
            device_id_type=MESH,
        )

    over(share_side, "start", 3)
    over(copy_c, "wait_recv")
    finish(recv_c, mixed, og, ct, out, gog)
    stores = [
        pltpu.make_async_copy(source, target, out_sem.at[i])
        for i, (source, target) in enumerate(
            [(out, out_hbm), (gog, gog_hbm), (gf, gf_hbm), (gig, gig_hbm), (gva, gva_hbm)]
        )
    ]
    stores[0].start()
    stores[1].start()
    over(share_side, "wait_recv", 3)
    total = lag_f[...].astype(F32)
    for j in range(3):
        total = total + lag_x[j].astype(F32)
    lag_g[pl.ds(my_y, 1)] = total.astype(BF16)[None]

    def gather_y(j):
        return pltpu.make_async_remote_copy(
            src_ref=lag_g.at[my_y],
            dst_ref=lag_g.at[my_y],
            send_sem=dp_send.at[3, j],
            recv_sem=dp_recv.at[3, j],
            device_id={"dp": y_peer(j)[1]},
            device_id_type=MESH,
        )

    over(gather_y, "start", 3)
    over(gather_y, "wait_recv", 3)
    for q in range(4):
        lag[:, q * QUARTER : (q + 1) * QUARTER] = lag_g[q]
    summed[...] = dot(perm[...], lag[...])

    def filter_row(r, carry):
        start = pl.multiple_of(r * N, N)
        piece = summed[pl.ds(pl.multiple_of(r * 16, 16), 16), :]
        gf[:, pl.ds(start, N)] = piece * envelope(start, N) * SCALE
        return carry

    lax.fori_loop(0, ROWS, filter_row, 0)
    stores[2].start()
    over(copy_u, "wait_recv")
    finish(recv_u, weighted, va, ig, gig, gva)
    stores[3].start()
    stores[4].start()
    for copy in (copy_t, copy_m, copy_w, copy_c, copy_z, copy_u):
        over(copy, "wait_send")
    for copy in (share_t, scatter_y, share_side, gather_y):
        over(copy, "wait_send", 3)
    for store in stores:
        store.wait()


def shards(input_gate, output_gate, values, cotangent, filter_raw, filter_decay, skip_gain):
    roots, turns = constant_tables()
    signal = pltpu.VMEM((32, LOCAL), BF16)
    blocks = pltpu.VMEM((2, CTX, ROWS, N), BF16)
    quarter = pltpu.VMEM((256, QUARTER), BF16)
    quarters = pltpu.VMEM((4, 256, QUARTER), BF16)
    big = jax.ShapeDtypeStruct((32, LOCAL), BF16)
    anywhere = pl.BlockSpec(memory_space=pl.ANY)
    outputs, grad_input_gate, grad_output_gate, grad_values, grad_filter = pl.pallas_call(
        kernel,
        out_shape=(big, big, big, big, jax.ShapeDtypeStruct((16, LOCAL), F32)),
        in_specs=[anywhere] * 9,
        out_specs=(anywhere,) * 5,
        scratch_shapes=[
            signal, signal, signal, signal,
            pltpu.VMEM((16, LOCAL), BF16),
            pltpu.VMEM((1, 16), F32),
            pltpu.VMEM((1, 32), F32),
            pltpu.VMEM((2, N, N), BF16),
            pltpu.VMEM((2, 48, N), F32),
            signal, signal, signal, signal,
            pltpu.VMEM((16, LOCAL), F32),
            pltpu.VMEM((2 * N, N), BF16),
            pltpu.VMEM((N, 2 * N), BF16),
            pltpu.VMEM((2 * N, 2 * N), BF16),
            pltpu.VMEM((2 * N, 2 * N), BF16),
            pltpu.VMEM((N, N), F32),
            pltpu.VMEM((N, N), F32),
            pltpu.VMEM((256, 256), BF16),
            pltpu.VMEM((2, 256, N), BF16),
            pltpu.VMEM((2, 256, N), BF16),
            blocks, blocks, blocks, blocks,
            quarter,
            quarters,
            pltpu.VMEM((256, N), BF16),
            pltpu.VMEM((N, 2 * N), BF16),
            pltpu.VMEM((N, 2 * N), F32),
            pltpu.VMEM((2 * N, N), BF16),
            pltpu.VMEM((2 * N, N), BF16),
            blocks, blocks, blocks, blocks,
            pltpu.VMEM((256, N), F32),
            quarters,
            quarters,
            quarter,
            quarter,
            pltpu.VMEM((3, 256, QUARTER), BF16),
            quarters,
            pltpu.VMEM((256, N), BF16),
            pltpu.SemaphoreType.DMA((9,)),
            pltpu.SemaphoreType.DMA((5,)),
            pltpu.SemaphoreType.DMA((6, CTX - 1)),
            pltpu.SemaphoreType.DMA((6, CTX - 1)),
            pltpu.SemaphoreType.DMA((4, 3)),
            pltpu.SemaphoreType.DMA((4, 3)),
        ],
        compiler_params=pltpu.CompilerParams(
            collective_id=0, has_side_effects=True, vmem_limit_bytes=60 << 20
        ),
    )(
        input_gate, values, cotangent, output_gate, filter_raw,
        filter_decay.reshape(1, 16), skip_gain.reshape(1, 32), jnp.asarray(roots), jnp.asarray(turns),
    )
    return outputs, grad_input_gate, grad_output_gate, grad_values, grad_filter


def solution(mesh):
    return jax.shard_map(
        shards,
        mesh=mesh,
        in_specs=(
            P("dp", "ctx"),
            P("dp", "ctx"),
            P("dp", "ctx"),
            P("dp", "ctx"),
            P(None, "ctx"),
            P(),
            P("dp"),
        ),
        out_specs=(P("dp", "ctx"), P("dp", "ctx"), P("dp", "ctx"), P("dp", "ctx"), P(None, "ctx")),
        check_vma=False,
    )
```

```python
import functools

import jax
import jax.numpy as jnp
import numpy as np
from jax import lax
from jax.experimental import pallas as pl
from jax.experimental.pallas import tpu as pltpu
from jax.sharding import PartitionSpec as P

N = 512
FFT_LEN = N * N
SEQ = FFT_LEN // 2
CTX = 16
ROWS = 16
LOCAL = ROWS * N
HALF = N // 2
QUARTER = N // 4
SCALE = SEQ**-0.5
CHUNK = 512
MESH = pl.DeviceIdType.MESH
F32 = jnp.float32
BF16 = jnp.bfloat16


def constant_tables():
    index = np.arange(N)
    angle = (index[:, None] * index[None, :] % N) * (2.0 * np.pi / N)
    roots = np.stack([np.cos(angle), np.sin(angle)]).astype(jnp.bfloat16)
    coarse = np.arange(N // ROWS)[:, None] * ROWS * index[None, :] * (2.0 * np.pi / FFT_LEN)
    fine = np.arange(ROWS)[:, None] * index[None, :] * (2.0 * np.pi / FFT_LEN)
    both = np.concatenate([coarse, fine], axis=0)
    turns = np.stack([np.cos(both), -np.sin(both)]).astype(np.float32)
    return roots, turns


def dot(left, right):
    return jnp.dot(left, right, preferred_element_type=F32)


def times(ar, ai, br, bi):
    return ar * br - ai * bi, ar * bi + ai * br


def conj_times(ar, ai, br, bi):
    return ar * br + ai * bi, ar * bi - ai * br


def joined(real, imaginary):
    return jnp.concatenate([real, imaginary], axis=1).astype(BF16)


def parts(value):
    return value[:, :N], value[:, N:]


def step_of(i):
    j = i // 2
    return 4 + (1 - 2 * (j % 2)) * ((j + 1) // 2), 1 - i % 2


def kernel(
    ig_hbm, va_hbm, ct_hbm, og_hbm, fr_hbm, decay_hbm, skip_hbm, roots_hbm, turns_hbm,
    out, gig, gog, gva, gf,
    ig, va, ct, og, fr, decay, skip, roots, turns,
    first, first_back, first_lag, first_taps, second, second_back, wr, wi, perm,
    mixed, weighted, send_m, recv_m, send_w, recv_w,
    send_t, taps_q, taps, spec_h, spec_m, spec_w, turned, turned_lag,
    send_c, recv_c, send_u, recv_u, summed,
    lag_q, lag_y, lag_z, lag_f, lag_g, lag,
    in_sem, ctx_send, ctx_recv, dp_send, dp_recv, lag_send, lag_recv,
):
    dp = lax.axis_index("dp")
    me = lax.axis_index("ctx")
    my_z, my_x = me // 2, me % 2
    place = dp % 8
    low, my_y, core = dp // 8, (dp // 2) % 4, dp % 2

    def ctx_peer(i):
        dz, dx = step_of(i)
        return ((my_z + dz) % 8) * 2 + (my_x + dx) % 2

    def plane_peer(j):
        place = (my_y * 2 + core + 1 + j) % 8
        return place, low * 8 + place

    def any_peer(i):
        moved = ctx_peer(i % (CTX - 1)) - me
        return (low + (i + 1) // CTX) % 2, me + moved * (1 - i // (2 * CTX - 2))

    barrier = pltpu.get_barrier_semaphore()

    def greet(i, carry):
        side, other = any_peer(i)
        device = (side * 8 + dp % 8, other)
        pl.semaphore_signal(barrier, inc=1, device_id=device, device_id_type=MESH)
        return carry

    def greet_plane(j, carry):
        pl.semaphore_signal(
            barrier, inc=1, device_id={"dp": plane_peer(j)[1]}, device_id_type=MESH
        )
        return carry

    lax.fori_loop(0, 2 * CTX - 1, greet, 0)
    lax.fori_loop(0, 7, greet_plane, 0)

    loads = [
        pltpu.make_async_copy(source, target, in_sem.at[i])
        for i, (source, target) in enumerate(
            [
                (ig_hbm, ig), (va_hbm, va), (decay_hbm, decay), (fr_hbm, fr), (ct_hbm, ct),
                (og_hbm, og), (roots_hbm, roots), (turns_hbm, turns), (skip_hbm, skip),
            ]
        )
    ]
    for load in loads:
        load.start()

    def selection(shape, where):
        row = lax.broadcasted_iota(jnp.int32, shape, 0)
        col = lax.broadcasted_iota(jnp.int32, shape, 1)
        return jnp.where(where(row, col), 1.0, 0.0).astype(BF16)

    perm[...] = selection((256, 256), lambda i, j: j == (i % 16) * 16 + i // 16)

    def column(line, count):
        r = lax.broadcasted_iota(jnp.int32, (count, count), 0)
        c = lax.broadcasted_iota(jnp.int32, (count, count), 1)
        return jnp.sum(jnp.where(r == c, line, 0.0), axis=1, keepdims=True)

    def multiply(left, right, target, send):
        for g in range(2):

            def block(r, carry, g=g):
                lanes = pl.ds(pl.multiple_of(r * N, N), N)
                a = left[g * 16 : g * 16 + 16, lanes].astype(F32)
                b = right[g * 16 : g * 16 + 16, lanes].astype(F32)
                target[g, pl.ds(pl.multiple_of(r * 16, 16), 16), :] = (a * b).astype(BF16)
                return carry

            lax.fori_loop(0, ROWS, block, 0)
            send[g] = dot(perm[...], target[g]).astype(BF16).reshape(16, 16, N)

    def exchange(k, send, recv):
        def copy(i):
            return pltpu.make_async_remote_copy(
                src_ref=send.at[:, ctx_peer(i)],
                dst_ref=recv.at[:, me],
                send_sem=ctx_send.at[k, i],
                recv_sem=ctx_recv.at[k, i],
                device_id={"ctx": ctx_peer(i)},
                device_id_type=MESH,
            )

        return copy

    def among(k, send, recv):
        def copy(j):
            return pltpu.make_async_remote_copy(
                src_ref=send(j),
                dst_ref=recv.at[place],
                send_sem=dp_send.at[k, j],
                recv_sem=dp_recv.at[k, j],
                device_id={"dp": plane_peer(j)[1]},
                device_id_type=MESH,
            )

        return copy

    def half_exchange(k, g, send, recv):
        def copy(i):
            return pltpu.make_async_remote_copy(
                src_ref=send.at[g, ctx_peer(i)],
                dst_ref=recv.at[g, me],
                send_sem=ctx_send.at[k, i],
                recv_sem=ctx_recv.at[k, i],
                device_id={"ctx": ctx_peer(i)},
                device_id_type=MESH,
            )

        return copy

    def small_exchange(k, send, recv):
        def copy(i):
            return pltpu.make_async_remote_copy(
                src_ref=send.at[ctx_peer(i)],
                dst_ref=recv.at[me],
                send_sem=ctx_send.at[k, i],
                recv_sem=ctx_recv.at[k, i],
                device_id={"ctx": ctx_peer(i)},
                device_id_type=MESH,
            )

        return copy

    def over(copy, action, count=CTX - 1, begin=0):
        def one(i, carry):
            getattr(copy(i), action)()
            return carry

        lax.fori_loop(begin, count, one, 0)

    def keep(send, recv):
        recv[:, pl.ds(me, 1)] = send[:, pl.ds(me, 1)]

    loads[2].wait()
    loads[3].wait()
    decay_column = column(decay[...], 16)

    def envelope(start, width):
        place = start + lax.broadcasted_iota(jnp.int32, (16, width), 1)
        place = (me * LOCAL + place).astype(F32)
        return jnp.exp(-decay_column * (place * (1.0 / SEQ)))

    def taps_row(r, carry):
        start = pl.multiple_of((core * 8 + r) * N + my_y * QUARTER, QUARTER)
        raw = fr[:, pl.ds(start, QUARTER)].astype(F32)
        made = (raw * envelope(start, QUARTER) * SCALE).astype(BF16)
        turned[pl.ds(pl.multiple_of(r * 16, 16), 16), 0:QUARTER] = made
        return carry

    lax.fori_loop(0, 8, taps_row, 0)
    swap = selection((128, 128), lambda i, j: j == (i % 8) * 16 + i // 8)
    arranged = dot(swap, turned[0:128, 0:QUARTER])
    send_t[...] = arranged.reshape(16, 8, QUARTER).astype(BF16)
    pl.semaphore_wait(barrier, 2 * CTX - 1 + 7)
    copy_t = small_exchange(0, send_t, taps_q.at[place])
    over(copy_t, "start")
    loads[0].wait()
    loads[1].wait()
    multiply(ig, va, mixed, send_m)
    copy_m = exchange(1, send_m, recv_m)
    over(copy_m, "start")
    loads[4].wait()
    loads[5].wait()
    multiply(ct, og, weighted, send_w)
    copy_w = exchange(2, send_w, recv_w)
    over(copy_w, "start")
    taps_q[pl.ds(place, 1), pl.ds(me, 1)] = send_t[pl.ds(me, 1)][None]
    keep(send_m, recv_m)
    keep(send_w, recv_w)

    loads[6].wait()
    loads[7].wait()
    loads[8].wait()
    cosine, sine = roots[0], roots[1]
    first[0:N, 0:HALF] = cosine[:, 0:HALF]
    first[0:N, HALF:N] = sine[:, 0:HALF]
    first[N:, 0:HALF] = -sine[:, 0:HALF]
    first[N:, HALF:N] = cosine[:, 0:HALF]
    first_back[0:HALF, 0:N] = cosine[0:HALF]
    first_back[0:HALF, N:] = -sine[0:HALF]
    first_back[HALF:, 0:N] = sine[0:HALF]
    first_back[HALF:, N:] = cosine[0:HALF]
    gather = selection(
        (256, 256), lambda i, j: j == ((i % 128) // 8) * 16 + (i // 128) * 8 + i % 8
    )
    scatter = selection(
        (256, 256), lambda i, j: i == ((j % 128) // 8) * 16 + (j // 128) * 8 + j % 8
    )
    first_taps[...] = dot(first[:, 0:HALF], scatter).astype(BF16)
    first_lag[...] = dot(gather, first_back[0:HALF, :]).astype(BF16)
    second[0:N, 0:N] = cosine
    second[0:N, N:] = -sine
    second[N:, 0:N] = sine
    second[N:, N:] = cosine
    second_back[0:N, 0:N] = cosine
    second_back[0:N, N:] = sine
    second_back[N:, 0:N] = -sine
    second_back[N:, N:] = cosine
    fine_r, fine_i = turns[0, 32:48, :], turns[1, 32:48, :]

    def turn_rows(a, carry):
        rows = pl.ds(pl.multiple_of(a * 16, 16), 16)
        tr, ti = times(turns[0, pl.ds(a, 1), :], turns[1, pl.ds(a, 1), :], fine_r, fine_i)
        wr[rows, :] = tr
        wi[rows, :] = ti
        return carry

    lax.fori_loop(0, N // 16, turn_rows, 0)

    over(copy_t, "wait_recv")

    share_t = among(0, lambda j: taps_q.at[place], taps_q)
    over(share_t, "start", 7)
    over(share_t, "wait_recv", 7)
    for p in range(8):
        y, half = p // 2, p % 2
        piece = taps_q[p].astype(F32).reshape(128, QUARTER).astype(BF16)
        taps[half * 128 : (half + 1) * 128, y * QUARTER : (y + 1) * QUARTER] = piece

    def forward(start, table, block):
        rows = pl.ds(start, CHUNK)
        pr = dot(table[rows, :], block)
        pi = dot(table[pl.ds(start + N, CHUNK), :], block)
        return dot(joined(*times(pr, pi, wr[rows, :], wi[rows, :])), second[...])

    def backward(start, spectrum, target):
        rows = pl.ds(start, CHUNK)
        br, bi = parts(dot(spectrum, second_back[...]))
        sr, si = conj_times(wr[rows, :], wi[rows, :], br, bi)
        target[rows, :] = (sr * (1.0 / FFT_LEN)).astype(BF16)
        target[pl.ds(start + N, CHUNK), :] = (si * (1.0 / FFT_LEN)).astype(BF16)

    def chunks(body):
        def one(i, carry):
            body(pl.multiple_of(i * CHUNK, CHUNK))
            return carry

        lax.fori_loop(0, N // CHUNK, one, 0)

    def filter_chunk(start):
        spec_h[pl.ds(start, CHUNK), :] = forward(start, first_taps, taps[...]).astype(BF16)

    chunks(filter_chunk)

    over(copy_m, "wait_recv")

    def mix_chunk(start):
        rows = pl.ds(start, CHUNK)
        spectrum = forward(start, first, recv_m[...].reshape(N, N))
        spec_m[rows, :] = spectrum
        hr, hi = parts(spec_h[rows, :].astype(F32))
        backward(start, joined(*times(*parts(spectrum), hr, hi)), turned)

    chunks(mix_chunk)
    for g in range(2):
        made = dot(first_back[g * HALF : (g + 1) * HALF, :], turned[...])
        send_c[g] = made.astype(BF16).reshape(16, 16, N)
    copy_c = exchange(3, send_c, recv_c)
    over(copy_c, "start")
    keep(send_c, recv_c)

    over(copy_w, "wait_recv")

    def weight_chunk(start):
        rows = pl.ds(start, CHUNK)
        spectrum = forward(start, first, recv_w[...].reshape(N, N))
        spec_w[rows, :] = spectrum
        mr, mi = parts(spec_m[rows, :])
        backward(start, joined(*conj_times(mr, mi, *parts(spectrum))), turned_lag)

    chunks(weight_chunk)
    lagged = dot(first_lag[...], turned_lag[...]).astype(BF16)
    for p in range(8):
        y, half = p // 2, p % 2
        lag_q[p] = lagged[half * 128 : (half + 1) * 128, y * QUARTER : (y + 1) * QUARTER]

    copy_s = among(1, lambda j: lag_q.at[plane_peer(j)[0]], lag_y)
    over(copy_s, "start", 7)
    lag_y[pl.ds(place, 1)] = lag_q[pl.ds(place, 1)]

    def correlate_chunk(start):
        rows = pl.ds(start, CHUNK)
        hr, hi = parts(spec_h[rows, :].astype(F32))
        backward(start, joined(*conj_times(hr, hi, *parts(spec_w[rows, :]))), turned)

    chunks(correlate_chunk)
    copy_u = [half_exchange(5 + g, g, send_u, recv_u) for g in range(2)]
    for g in range(2):
        made = dot(first_back[g * HALF : (g + 1) * HALF, :], turned[...])
        send_u[g] = made.astype(BF16).reshape(16, 16, N)
        if g == 0:
            over(copy_u[0], "start", 8)
    over(copy_s, "wait_recv", 7)
    reduced = sum(lag_y[p].astype(F32) for p in range(8))
    lag_z[...] = reduced.reshape(16, 8, QUARTER).astype(BF16)

    def copy_z(i):
        side, other = any_peer(i)
        return pltpu.make_async_remote_copy(
            src_ref=lag_z.at[other],
            dst_ref=lag_f.at[low, me],
            send_sem=lag_send.at[i],
            recv_sem=lag_recv.at[i],
            device_id=(side * 8 + place, other),
            device_id_type=MESH,
        )

    over(copy_z, "start", 2 * CTX - 1)
    over(copy_u[0], "start", begin=8)
    over(copy_u[1], "start")
    lag_f[pl.ds(low, 1), pl.ds(me, 1)] = lag_z[pl.ds(me, 1)][None]
    keep(send_u, recv_u)

    skip_column = column(skip[...], 32)

    def finish(g, recv, base, left, right, first_out, second_out):
        gain = skip_column[g * 16 : g * 16 + 16]
        summed[...] = dot(perm[...], recv[g].reshape(256, N))

        def block(r, carry):
            rows = pl.ds(pl.multiple_of(r * 16, 16), 16)
            lanes = pl.ds(pl.multiple_of(r * N, N), N)
            total = summed[rows, :] + gain * base[g, rows, :].astype(F32)
            place = slice(g * 16, g * 16 + 16)
            first_out[place, lanes] = (left[place, lanes].astype(F32) * total).astype(BF16)
            second_out[place, lanes] = (right[place, lanes].astype(F32) * total).astype(BF16)
            return carry

        lax.fori_loop(0, ROWS, block, 0)

    over(copy_c, "wait_recv")
    for g in range(2):
        finish(g, recv_c, mixed, og, ct, out, gog)
    over(copy_z, "wait_recv", 2 * CTX - 1)
    both = lag_f[0].astype(F32) + lag_f[1].astype(F32)
    lag_g[pl.ds(place, 1)] = both.reshape(128, QUARTER).astype(BF16)[None]
    copy_g = among(2, lambda j: lag_g.at[place], lag_g)
    over(copy_g, "start", 7)
    over(copy_u[0], "wait_recv")
    finish(0, recv_u, weighted, va, ig, gig, gva)
    over(copy_g, "wait_recv", 7)
    for p in range(8):
        y, half = p // 2, p % 2
        lag[half * 128 : (half + 1) * 128, y * QUARTER : (y + 1) * QUARTER] = lag_g[p]
    order = selection(
        (256, 256), lambda i, j: j == (i // 128) * 128 + (i % 16) * 8 + (i % 128) // 16
    )
    summed[...] = dot(order, lag[...])

    def filter_row(r, carry):
        start = pl.multiple_of(r * N, N)
        piece = summed[pl.ds(pl.multiple_of(r * 16, 16), 16), :]
        gf[:, pl.ds(start, N)] = piece * envelope(start, N) * SCALE
        return carry

    lax.fori_loop(0, ROWS, filter_row, 0)
    over(copy_u[1], "wait_recv")
    finish(1, recv_u, weighted, va, ig, gig, gva)
    for copy in (copy_t, copy_m, copy_w, copy_c, *copy_u):
        over(copy, "wait_send")
    for copy in (copy_s, copy_g):
        over(copy, "wait_send", 7)
    over(copy_z, "wait_send", 2 * CTX - 1)
    over(share_t, "wait_send", 7)


def store_kernel(*refs):
    copies = [
        pltpu.make_async_copy(source, target, refs[10].at[i])
        for i, (source, target) in enumerate(zip(refs[:5], refs[5:10]))
    ]
    for copy in copies:
        copy.start()
    for copy in copies:
        copy.wait()


def shards(input_gate, output_gate, values, cotangent, filter_raw, filter_decay, skip_gain):
    roots, turns = constant_tables()
    signal = pltpu.VMEM((32, LOCAL), BF16)
    blocks = pltpu.VMEM((2, CTX, ROWS, N), BF16)
    pieces = pltpu.VMEM((8, 128, QUARTER), BF16)
    kept = pltpu.VMEM((16, LOCAL), F32)
    inside = pl.BlockSpec(memory_space=pltpu.VMEM)
    anywhere = pl.BlockSpec(memory_space=pl.ANY)
    made = pl.pallas_call(
        kernel,
        out_shape=(signal, signal, signal, signal, kept),
        in_specs=[pl.BlockSpec(memory_space=pltpu.HBM)] * 9,
        out_specs=(inside,) * 5,
        scratch_shapes=[
            signal, signal, signal, signal,
            pltpu.VMEM((16, LOCAL), BF16),
            pltpu.VMEM((1, 16), F32),
            pltpu.VMEM((1, 32), F32),
            pltpu.VMEM((2, N, N), BF16),
            pltpu.VMEM((2, 48, N), F32),
            pltpu.VMEM((2 * N, N), BF16),
            pltpu.VMEM((N, 2 * N), BF16),
            pltpu.VMEM((HALF, 2 * N), BF16),
            pltpu.VMEM((2 * N, HALF), BF16),
            pltpu.VMEM((2 * N, 2 * N), BF16),
            pltpu.VMEM((2 * N, 2 * N), BF16),
            pltpu.VMEM((N, N), F32),
            pltpu.VMEM((N, N), F32),
            pltpu.VMEM((256, 256), BF16),
            pltpu.VMEM((2, 256, N), BF16),
            pltpu.VMEM((2, 256, N), BF16),
            blocks, blocks, blocks, blocks,
            pltpu.VMEM((CTX, 8, QUARTER), BF16),
            pltpu.VMEM((8, CTX, 8, QUARTER), BF16),
            pltpu.VMEM((256, N), BF16),
            pltpu.VMEM((N, 2 * N), BF16),
            pltpu.VMEM((N, 2 * N), F32),
            pltpu.VMEM((N, 2 * N), F32),
            pltpu.VMEM((2 * N, N), BF16),
            pltpu.VMEM((2 * N, N), BF16),
            blocks, blocks, blocks, blocks,
            pltpu.VMEM((256, N), F32),
            pieces,
            pieces,
            pltpu.VMEM((CTX, 8, QUARTER), BF16),
            pltpu.VMEM((2, CTX, 8, QUARTER), BF16),
            pieces,
            pltpu.VMEM((256, N), BF16),
            pltpu.SemaphoreType.DMA((9,)),
            pltpu.SemaphoreType.DMA((7, CTX - 1)),
            pltpu.SemaphoreType.DMA((7, CTX - 1)),
            pltpu.SemaphoreType.DMA((3, 7)),
            pltpu.SemaphoreType.DMA((3, 7)),
            pltpu.SemaphoreType.DMA((2 * CTX - 1,)),
            pltpu.SemaphoreType.DMA((2 * CTX - 1,)),
        ],
        compiler_params=pltpu.CompilerParams(
            collective_id=0, has_side_effects=True, vmem_limit_bytes=48 << 20
        ),
    )(
        *[
            pltpu.with_memory_space_constraint(x, pltpu.HBM)
            for x in (
                input_gate, values, cotangent, output_gate, filter_raw,
                filter_decay.reshape(1, 16), skip_gain.reshape(1, 32), jnp.asarray(roots), jnp.asarray(turns),
            )
        ]
    )
    big = jax.ShapeDtypeStruct((32, LOCAL), BF16)
    return pl.pallas_call(
        store_kernel,
        out_shape=(big, big, big, big, jax.ShapeDtypeStruct((16, LOCAL), F32)),
        in_specs=[inside] * 5,
        out_specs=(anywhere,) * 5,
        scratch_shapes=[pltpu.SemaphoreType.DMA((5,))],
        compiler_params=pltpu.CompilerParams(vmem_limit_bytes=8 << 20),
    )(*made)


def solution(mesh):
    return jax.shard_map(
        shards,
        mesh=mesh,
        in_specs=(
            P("dp", "ctx"),
            P("dp", "ctx"),
            P("dp", "ctx"),
            P("dp", "ctx"),
            P(None, "ctx"),
            P(),
            P("dp"),
        ),
        out_specs=(P("dp", "ctx"), P("dp", "ctx"), P("dp", "ctx"), P("dp", "ctx"), P(None, "ctx")),
        check_vma=False,
    )
```

```python
import functools

import jax
import jax.numpy as jnp
import numpy as np
from jax import lax
from jax.experimental import pallas as pl
from jax.experimental.pallas import tpu as pltpu
from jax.sharding import PartitionSpec as P

N = 512
FFT_LEN = N * N
SEQ = FFT_LEN // 2
CTX = 16
ROWS = 16
LOCAL = ROWS * N
HALF = N // 2
QUARTER = N // 4
SCALE = SEQ**-0.5
CHUNK = 512
MESH = pl.DeviceIdType.MESH
F32 = jnp.float32
BF16 = jnp.bfloat16


def constant_tables():
    index = np.arange(N)
    angle = (index[:, None] * index[None, :] % N) * (2.0 * np.pi / N)
    roots = np.stack([np.cos(angle), np.sin(angle)]).astype(jnp.bfloat16)
    coarse = np.arange(N // ROWS)[:, None] * ROWS * index[None, :] * (2.0 * np.pi / FFT_LEN)
    fine = np.arange(ROWS)[:, None] * index[None, :] * (2.0 * np.pi / FFT_LEN)
    both = np.concatenate([coarse, fine], axis=0)
    turns = np.stack([np.cos(both), -np.sin(both)]).astype(np.float32)
    return roots, turns


def dot(left, right):
    return jnp.dot(left, right, preferred_element_type=F32)


def times(ar, ai, br, bi):
    return ar * br - ai * bi, ar * bi + ai * br


def conj_times(ar, ai, br, bi):
    return ar * br + ai * bi, ar * bi - ai * br


def joined(real, imaginary):
    return jnp.concatenate([real, imaginary], axis=1).astype(BF16)


def parts(value):
    return value[:, :N], value[:, N:]


def step_of(i):
    j = i // 2
    return 4 + (1 - 2 * (j % 2)) * ((j + 1) // 2), 1 - i % 2


def kernel(
    ig_hbm, va_hbm, ct_hbm, og_hbm, fr_hbm, decay_hbm, skip_hbm, roots_hbm, turns_hbm,
    out, gig, gog, gva, gf,
    ig, va, ct, og, fr, decay, skip, roots, turns,
    first, first_back, first_lag, first_taps, second, second_back, wr, wi, perm,
    mixed, weighted, send_m, recv_m, send_w, recv_w,
    send_t, taps_q, taps, spec_h, spec_m, spec_w, turned, turned_lag,
    send_c, recv_c, send_u, recv_u, summed,
    lag_q, lag_y, lag_z, lag_f, lag_g, lag,
    in_sem, ctx_send, ctx_recv, dp_send, dp_recv, lag_send, lag_recv,
):
    dp = lax.axis_index("dp")
    me = lax.axis_index("ctx")
    my_z, my_x = me // 2, me % 2
    place = dp % 8
    low, my_y, core = dp // 8, (dp // 2) % 4, dp % 2

    def ctx_peer(i):
        dz, dx = step_of(i)
        return ((my_z + dz) % 8) * 2 + (my_x + dx) % 2

    def plane_peer(j):
        place = (my_y * 2 + core + 1 + j) % 8
        return place, low * 8 + place

    def any_peer(i):
        moved = ctx_peer(i % (CTX - 1)) - me
        return (low + (i + 1) // CTX) % 2, me + moved * (1 - i // (2 * CTX - 2))

    loads = [
        pltpu.make_async_copy(source, target, in_sem.at[i])
        for i, (source, target) in enumerate(
            [
                (ig_hbm, ig), (va_hbm, va), (decay_hbm, decay), (fr_hbm, fr), (ct_hbm, ct),
                (og_hbm, og), (roots_hbm, roots), (turns_hbm, turns), (skip_hbm, skip),
            ]
        )
    ]
    for load in loads:
        load.start()

    barrier = pltpu.get_barrier_semaphore()

    def greet(i, carry):
        side, other = any_peer(i)
        device = (side * 8 + dp % 8, other)
        pl.semaphore_signal(barrier, inc=1, device_id=device, device_id_type=MESH)
        return carry

    def greet_plane(j, carry):
        pl.semaphore_signal(
            barrier, inc=1, device_id={"dp": plane_peer(j)[1]}, device_id_type=MESH
        )
        return carry

    lax.fori_loop(0, 2 * CTX - 1, greet, 0)
    lax.fori_loop(0, 7, greet_plane, 0)

    def selection(shape, where):
        row = lax.broadcasted_iota(jnp.int32, shape, 0)
        col = lax.broadcasted_iota(jnp.int32, shape, 1)
        return jnp.where(where(row, col), 1.0, 0.0).astype(BF16)

    perm[...] = selection((256, 256), lambda i, j: j == (i % 16) * 16 + i // 16)

    def column(line, count):
        r = lax.broadcasted_iota(jnp.int32, (count, count), 0)
        c = lax.broadcasted_iota(jnp.int32, (count, count), 1)
        return jnp.sum(jnp.where(r == c, line, 0.0), axis=1, keepdims=True)

    def multiply(left, right, target, send):
        for g in range(2):

            def block(r, carry, g=g):
                lanes = pl.ds(pl.multiple_of(r * N, N), N)
                a = left[g * 16 : g * 16 + 16, lanes].astype(F32)
                b = right[g * 16 : g * 16 + 16, lanes].astype(F32)
                target[g, pl.ds(pl.multiple_of(r * 16, 16), 16), :] = (a * b).astype(BF16)
                return carry

            lax.fori_loop(0, ROWS, block, 0, unroll=4)
            send[g] = dot(perm[...], target[g]).astype(BF16).reshape(16, 16, N)

    def exchange(k, send, recv):
        def copy(i):
            return pltpu.make_async_remote_copy(
                src_ref=send.at[:, ctx_peer(i)],
                dst_ref=recv.at[:, me],
                send_sem=ctx_send.at[k, i],
                recv_sem=ctx_recv.at[k, i],
                device_id={"ctx": ctx_peer(i)},
                device_id_type=MESH,
            )

        return copy

    def among(k, send, recv):
        def copy(j):
            return pltpu.make_async_remote_copy(
                src_ref=send(j),
                dst_ref=recv.at[place],
                send_sem=dp_send.at[k, j],
                recv_sem=dp_recv.at[k, j],
                device_id={"dp": plane_peer(j)[1]},
                device_id_type=MESH,
            )

        return copy

    def half_exchange(k, g, send, recv):
        def copy(i):
            return pltpu.make_async_remote_copy(
                src_ref=send.at[g, ctx_peer(i)],
                dst_ref=recv.at[g, me],
                send_sem=ctx_send.at[k, i],
                recv_sem=ctx_recv.at[k, i],
                device_id={"ctx": ctx_peer(i)},
                device_id_type=MESH,
            )

        return copy

    def small_exchange(k, send, recv):
        def copy(i):
            return pltpu.make_async_remote_copy(
                src_ref=send.at[ctx_peer(i)],
                dst_ref=recv.at[me],
                send_sem=ctx_send.at[k, i],
                recv_sem=ctx_recv.at[k, i],
                device_id={"ctx": ctx_peer(i)},
                device_id_type=MESH,
            )

        return copy

    def over(copy, action, count=CTX - 1, begin=0):
        def one(i, carry):
            getattr(copy(i), action)()
            return carry

        lax.fori_loop(begin, count, one, 0)

    def keep(send, recv):
        recv[:, pl.ds(me, 1)] = send[:, pl.ds(me, 1)]

    loads[2].wait()
    loads[3].wait()
    decay_column = column(decay[...], 16)

    def envelope(start, width):
        place = start + lax.broadcasted_iota(jnp.int32, (16, width), 1)
        place = (me * LOCAL + place).astype(F32)
        return jnp.exp(-decay_column * (place * (1.0 / SEQ)))

    def taps_row(r, carry):
        start = pl.multiple_of((core * 8 + r) * N + my_y * QUARTER, QUARTER)
        raw = fr[:, pl.ds(start, QUARTER)].astype(F32)
        made = (raw * envelope(start, QUARTER) * SCALE).astype(BF16)
        turned[pl.ds(pl.multiple_of(r * 16, 16), 16), 0:QUARTER] = made
        return carry

    lax.fori_loop(0, 8, taps_row, 0)
    swap = selection((128, 128), lambda i, j: j == (i % 8) * 16 + i // 8)
    arranged = dot(swap, turned[0:128, 0:QUARTER])
    send_t[...] = arranged.reshape(16, 8, QUARTER).astype(BF16)
    pl.semaphore_wait(barrier, 2 * CTX - 1 + 7)
    copy_t = small_exchange(0, send_t, taps_q.at[place])
    over(copy_t, "start")
    loads[0].wait()
    loads[1].wait()
    multiply(ig, va, mixed, send_m)
    copy_m = exchange(1, send_m, recv_m)
    over(copy_m, "start")
    loads[4].wait()
    loads[5].wait()
    multiply(ct, og, weighted, send_w)
    copy_w = exchange(2, send_w, recv_w)
    over(copy_w, "start")
    taps_q[pl.ds(place, 1), pl.ds(me, 1)] = send_t[pl.ds(me, 1)][None]
    keep(send_m, recv_m)
    keep(send_w, recv_w)

    loads[6].wait()
    loads[7].wait()
    loads[8].wait()
    cosine, sine = roots[0], roots[1]
    first[0:N, 0:HALF] = cosine[:, 0:HALF]
    first[0:N, HALF:N] = sine[:, 0:HALF]
    first[N:, 0:HALF] = -sine[:, 0:HALF]
    first[N:, HALF:N] = cosine[:, 0:HALF]
    first_back[0:HALF, 0:N] = cosine[0:HALF]
    first_back[0:HALF, N:] = -sine[0:HALF]
    first_back[HALF:, 0:N] = sine[0:HALF]
    first_back[HALF:, N:] = cosine[0:HALF]
    gather = selection(
        (256, 256), lambda i, j: j == ((i % 128) // 8) * 16 + (i // 128) * 8 + i % 8
    )
    scatter = selection(
        (256, 256), lambda i, j: i == ((j % 128) // 8) * 16 + (j // 128) * 8 + j % 8
    )
    first_taps[...] = dot(first[:, 0:HALF], scatter).astype(BF16)
    first_lag[...] = dot(gather, first_back[0:HALF, :]).astype(BF16)
    second[0:N, 0:N] = cosine
    second[0:N, N:] = -sine
    second[N:, 0:N] = sine
    second[N:, N:] = cosine
    second_back[0:N, 0:N] = cosine
    second_back[0:N, N:] = sine
    second_back[N:, 0:N] = -sine
    second_back[N:, N:] = cosine
    fine_r, fine_i = turns[0, 32:48, :], turns[1, 32:48, :]

    def turn_rows(a, carry):
        rows = pl.ds(pl.multiple_of(a * 16, 16), 16)
        tr, ti = times(turns[0, pl.ds(a, 1), :], turns[1, pl.ds(a, 1), :], fine_r, fine_i)
        wr[rows, :] = tr
        wi[rows, :] = ti
        return carry

    lax.fori_loop(0, N // 16, turn_rows, 0)

    over(copy_t, "wait_recv")

    share_t = among(0, lambda j: taps_q.at[place], taps_q)
    over(share_t, "start", 7)
    over(share_t, "wait_recv", 7)
    for p in range(8):
        y, half = p // 2, p % 2
        piece = taps_q[p].astype(F32).reshape(128, QUARTER).astype(BF16)
        taps[half * 128 : (half + 1) * 128, y * QUARTER : (y + 1) * QUARTER] = piece

    def forward(start, table, block):
        rows = pl.ds(start, CHUNK)
        pr = dot(table[rows, :], block)
        pi = dot(table[pl.ds(start + N, CHUNK), :], block)
        return dot(joined(*times(pr, pi, wr[rows, :], wi[rows, :])), second[...])

    def backward(start, spectrum, target):
        rows = pl.ds(start, CHUNK)
        br, bi = parts(dot(spectrum, second_back[...]))
        sr, si = conj_times(wr[rows, :], wi[rows, :], br, bi)
        target[rows, :] = (sr * (1.0 / FFT_LEN)).astype(BF16)
        target[pl.ds(start + N, CHUNK), :] = (si * (1.0 / FFT_LEN)).astype(BF16)

    def chunks(body):
        def one(i, carry):
            body(pl.multiple_of(i * CHUNK, CHUNK))
            return carry

        lax.fori_loop(0, N // CHUNK, one, 0)

    def filter_chunk(start):
        spec_h[pl.ds(start, CHUNK), :] = forward(start, first_taps, taps[...]).astype(BF16)

    chunks(filter_chunk)

    over(copy_m, "wait_recv")

    def mix_chunk(start):
        rows = pl.ds(start, CHUNK)
        spectrum = forward(start, first, recv_m[...].reshape(N, N))
        spec_m[rows, :] = spectrum
        hr, hi = parts(spec_h[rows, :].astype(F32))
        backward(start, joined(*times(*parts(spectrum), hr, hi)), turned)

    chunks(mix_chunk)
    for g in range(2):
        made = dot(first_back[g * HALF : (g + 1) * HALF, :], turned[...])
        send_c[g] = made.astype(BF16).reshape(16, 16, N)
    copy_c = exchange(3, send_c, recv_c)
    over(copy_c, "start")
    keep(send_c, recv_c)

    over(copy_w, "wait_recv")

    def weight_chunk(start):
        rows = pl.ds(start, CHUNK)
        spectrum = forward(start, first, recv_w[...].reshape(N, N))
        spec_w[rows, :] = spectrum
        mr, mi = parts(spec_m[rows, :])
        backward(start, joined(*conj_times(mr, mi, *parts(spectrum))), turned_lag)

    chunks(weight_chunk)
    lagged = dot(first_lag[...], turned_lag[...]).astype(BF16)
    for p in range(8):
        y, half = p // 2, p % 2
        lag_q[p] = lagged[half * 128 : (half + 1) * 128, y * QUARTER : (y + 1) * QUARTER]

    copy_s = among(1, lambda j: lag_q.at[plane_peer(j)[0]], lag_y)
    over(copy_s, "start", 7)
    lag_y[pl.ds(place, 1)] = lag_q[pl.ds(place, 1)]

    def correlate_chunk(start):
        rows = pl.ds(start, CHUNK)
        hr, hi = parts(spec_h[rows, :].astype(F32))
        backward(start, joined(*conj_times(hr, hi, *parts(spec_w[rows, :]))), turned)

    chunks(correlate_chunk)
    copy_u = [half_exchange(5 + g, g, send_u, recv_u) for g in range(2)]
    for g in range(2):
        made = dot(first_back[g * HALF : (g + 1) * HALF, :], turned[...])
        send_u[g] = made.astype(BF16).reshape(16, 16, N)
        if g == 0:
            over(copy_u[0], "start", 8)
    over(copy_s, "wait_recv", 7)
    reduced = sum(lag_y[p].astype(F32) for p in range(8))
    lag_z[...] = reduced.reshape(16, 8, QUARTER).astype(BF16)

    def copy_z(i):
        side, other = any_peer(i)
        return pltpu.make_async_remote_copy(
            src_ref=lag_z.at[other],
            dst_ref=lag_f.at[low, me],
            send_sem=lag_send.at[i],
            recv_sem=lag_recv.at[i],
            device_id=(side * 8 + place, other),
            device_id_type=MESH,
        )

    over(copy_z, "start", 2 * CTX - 1)
    over(copy_u[0], "start", begin=8)
    over(copy_u[1], "start")
    lag_f[pl.ds(low, 1), pl.ds(me, 1)] = lag_z[pl.ds(me, 1)][None]
    keep(send_u, recv_u)

    skip_column = column(skip[...], 32)

    def finish(g, recv, base, left, right, first_out, second_out):
        gain = skip_column[g * 16 : g * 16 + 16]
        summed[...] = dot(perm[...], recv[g].reshape(256, N))

        def block(r, carry):
            rows = pl.ds(pl.multiple_of(r * 16, 16), 16)
            lanes = pl.ds(pl.multiple_of(r * N, N), N)
            total = summed[rows, :] + gain * base[g, rows, :].astype(F32)
            place = slice(g * 16, g * 16 + 16)
            first_out[place, lanes] = (left[place, lanes].astype(F32) * total).astype(BF16)
            second_out[place, lanes] = (right[place, lanes].astype(F32) * total).astype(BF16)
            return carry

        lax.fori_loop(0, ROWS, block, 0, unroll=4)

    over(copy_c, "wait_recv")
    for g in range(2):
        finish(g, recv_c, mixed, og, ct, out, gog)
    over(copy_z, "wait_recv", 2 * CTX - 1)
    both = lag_f[0].astype(F32) + lag_f[1].astype(F32)
    lag_g[pl.ds(place, 1)] = both.reshape(128, QUARTER).astype(BF16)[None]
    copy_g = among(2, lambda j: lag_g.at[place], lag_g)
    over(copy_g, "start", 7)
    over(copy_u[0], "wait_recv")
    finish(0, recv_u, weighted, va, ig, gig, gva)
    over(copy_g, "wait_recv", 7)
    for p in range(8):
        y, half = p // 2, p % 2
        lag[half * 128 : (half + 1) * 128, y * QUARTER : (y + 1) * QUARTER] = lag_g[p]
    order = selection(
        (256, 256), lambda i, j: j == (i // 128) * 128 + (i % 16) * 8 + (i % 128) // 16
    )
    summed[...] = dot(order, lag[...])

    def filter_row(r, carry):
        start = pl.multiple_of(r * N, N)
        piece = summed[pl.ds(pl.multiple_of(r * 16, 16), 16), :]
        gf[:, pl.ds(start, N)] = piece * envelope(start, N) * SCALE
        return carry

    lax.fori_loop(0, ROWS, filter_row, 0)
    for copy in (copy_t, copy_m, copy_w, copy_c, *copy_u):
        over(copy, "wait_send")
    for copy in (copy_s, copy_g, share_t):
        over(copy, "wait_send", 7)
    over(copy_z, "wait_send", 2 * CTX - 1)
    over(copy_u[1], "wait_recv")
    finish(1, recv_u, weighted, va, ig, gig, gva)


def store_kernel(*refs):
    copies = [
        pltpu.make_async_copy(source, target, refs[10].at[i])
        for i, (source, target) in enumerate(zip(refs[:5], refs[5:10]))
    ]
    for copy in copies:
        copy.start()
    for copy in copies:
        copy.wait()


def shards(input_gate, output_gate, values, cotangent, filter_raw, filter_decay, skip_gain):
    roots, turns = constant_tables()
    signal = pltpu.VMEM((32, LOCAL), BF16)
    blocks = pltpu.VMEM((2, CTX, ROWS, N), BF16)
    pieces = pltpu.VMEM((8, 128, QUARTER), BF16)
    kept = pltpu.VMEM((16, LOCAL), F32)
    inside = pl.BlockSpec(memory_space=pltpu.VMEM)
    anywhere = pl.BlockSpec(memory_space=pl.ANY)
    made = pl.pallas_call(
        kernel,
        out_shape=(signal, signal, signal, signal, kept),
        in_specs=[pl.BlockSpec(memory_space=pltpu.HBM)] * 9,
        out_specs=(inside,) * 5,
        scratch_shapes=[
            signal, signal, signal, signal,
            pltpu.VMEM((16, LOCAL), BF16),
            pltpu.VMEM((1, 16), F32),
            pltpu.VMEM((1, 32), F32),
            pltpu.VMEM((2, N, N), BF16),
            pltpu.VMEM((2, 48, N), F32),
            pltpu.VMEM((2 * N, N), BF16),
            pltpu.VMEM((N, 2 * N), BF16),
            pltpu.VMEM((HALF, 2 * N), BF16),
            pltpu.VMEM((2 * N, HALF), BF16),
            pltpu.VMEM((2 * N, 2 * N), BF16),
            pltpu.VMEM((2 * N, 2 * N), BF16),
            pltpu.VMEM((N, N), F32),
            pltpu.VMEM((N, N), F32),
            pltpu.VMEM((256, 256), BF16),
            pltpu.VMEM((2, 256, N), BF16),
            pltpu.VMEM((2, 256, N), BF16),
            blocks, blocks, blocks, blocks,
            pltpu.VMEM((CTX, 8, QUARTER), BF16),
            pltpu.VMEM((8, CTX, 8, QUARTER), BF16),
            pltpu.VMEM((256, N), BF16),
            pltpu.VMEM((N, 2 * N), BF16),
            pltpu.VMEM((N, 2 * N), F32),
            pltpu.VMEM((N, 2 * N), F32),
            pltpu.VMEM((2 * N, N), BF16),
            pltpu.VMEM((2 * N, N), BF16),
            blocks, blocks, blocks, blocks,
            pltpu.VMEM((256, N), F32),
            pieces,
            pieces,
            pltpu.VMEM((CTX, 8, QUARTER), BF16),
            pltpu.VMEM((2, CTX, 8, QUARTER), BF16),
            pieces,
            pltpu.VMEM((256, N), BF16),
            pltpu.SemaphoreType.DMA((9,)),
            pltpu.SemaphoreType.DMA((7, CTX - 1)),
            pltpu.SemaphoreType.DMA((7, CTX - 1)),
            pltpu.SemaphoreType.DMA((3, 7)),
            pltpu.SemaphoreType.DMA((3, 7)),
            pltpu.SemaphoreType.DMA((2 * CTX - 1,)),
            pltpu.SemaphoreType.DMA((2 * CTX - 1,)),
        ],
        compiler_params=pltpu.CompilerParams(
            collective_id=0, has_side_effects=True, vmem_limit_bytes=48 << 20
        ),
    )(
        *[
            pltpu.with_memory_space_constraint(x, pltpu.HBM)
            for x in (
                input_gate, values, cotangent, output_gate, filter_raw,
                filter_decay.reshape(1, 16), skip_gain.reshape(1, 32), jnp.asarray(roots), jnp.asarray(turns),
            )
        ]
    )
    big = jax.ShapeDtypeStruct((32, LOCAL), BF16)
    return pl.pallas_call(
        store_kernel,
        out_shape=(big, big, big, big, jax.ShapeDtypeStruct((16, LOCAL), F32)),
        in_specs=[inside] * 5,
        out_specs=(anywhere,) * 5,
        scratch_shapes=[pltpu.SemaphoreType.DMA((5,))],
        compiler_params=pltpu.CompilerParams(vmem_limit_bytes=8 << 20),
    )(*made)


def solution(mesh):
    return jax.shard_map(
        shards,
        mesh=mesh,
        in_specs=(
            P("dp", "ctx"),
            P("dp", "ctx"),
            P("dp", "ctx"),
            P("dp", "ctx"),
            P(None, "ctx"),
            P(),
            P("dp"),
        ),
        out_specs=(P("dp", "ctx"), P("dp", "ctx"), P("dp", "ctx"), P("dp", "ctx"), P(None, "ctx")),
        check_vma=False,
    )
```

```python
import functools

import jax
import jax.numpy as jnp
import numpy as np
from jax import lax
from jax.experimental import pallas as pl
from jax.experimental.pallas import tpu as pltpu
from jax.sharding import PartitionSpec as P

N = 512
FFT_LEN = N * N
SEQ = FFT_LEN // 2
CTX = 16
ROWS = 16
LOCAL = ROWS * N
HALF = N // 2
QUARTER = N // 4
SCALE = SEQ**-0.5
CHUNK = 512
MESH = pl.DeviceIdType.MESH
F32 = jnp.float32
BF16 = jnp.bfloat16


def constant_tables():
    index = np.arange(N)
    angle = (index[:, None] * index[None, :] % N) * (2.0 * np.pi / N)
    roots = np.stack([np.cos(angle), np.sin(angle)]).astype(jnp.bfloat16)
    coarse = np.arange(N // ROWS)[:, None] * ROWS * index[None, :] * (2.0 * np.pi / FFT_LEN)
    fine = np.arange(ROWS)[:, None] * index[None, :] * (2.0 * np.pi / FFT_LEN)
    both = np.concatenate([coarse, fine], axis=0)
    turns = np.stack([np.cos(both), -np.sin(both)]).astype(np.float32)
    return roots, turns


def dot(left, right):
    return jnp.dot(left, right, preferred_element_type=F32)


def times(ar, ai, br, bi):
    return ar * br - ai * bi, ar * bi + ai * br


def conj_times(ar, ai, br, bi):
    return ar * br + ai * bi, ar * bi - ai * br


def joined(real, imaginary):
    return jnp.concatenate([real, imaginary], axis=1).astype(BF16)


def parts(value):
    return value[:, :N], value[:, N:]


def step_of(i):
    j = i // 2
    return 4 + (1 - 2 * (j % 2)) * ((j + 1) // 2), 1 - i % 2


def kernel(
    ig_hbm, va_hbm, ct_hbm, og_hbm, fr_hbm, decay_hbm, skip_hbm, roots_hbm, turns_hbm,
    out, gig, gog, gva, gf,
    ig, va, ct, og, fr, decay, skip, roots, turns,
    first, first_back, first_lag, first_taps, second, second_back, wr, wi, perm,
    mixed, weighted, send_m, recv_m, send_w, recv_w,
    send_t, taps_q, taps, spec_h, spec_m, spec_w, turned, turned_lag,
    send_c, recv_c, send_u, recv_u, summed,
    lag_q, lag_y, lag_z, lag_f, lag_g, lag,
    in_sem, ctx_send, ctx_recv, dp_send, dp_recv, lag_send, lag_recv,
):
    dp = lax.axis_index("dp")
    me = lax.axis_index("ctx")
    my_z, my_x = me // 2, me % 2
    place = dp % 8
    low, my_y, core = dp // 8, (dp // 2) % 4, dp % 2

    def ctx_peer(i):
        dz, dx = step_of(i)
        return ((my_z + dz) % 8) * 2 + (my_x + dx) % 2

    def plane_peer(j):
        place = (my_y * 2 + core + 1 + j) % 8
        return place, low * 8 + place

    def any_peer(i):
        moved = ctx_peer(i % (CTX - 1)) - me
        return (low + (i + 1) // CTX) % 2, me + moved * (1 - i // (2 * CTX - 2))

    loads = [
        pltpu.make_async_copy(source, target, in_sem.at[i])
        for i, (source, target) in enumerate(
            [
                (ig_hbm, ig), (va_hbm, va), (decay_hbm, decay), (fr_hbm, fr), (ct_hbm, ct),
                (og_hbm, og), (roots_hbm, roots), (turns_hbm, turns), (skip_hbm, skip),
            ]
        )
    ]
    for load in loads:
        load.start()

    barrier = pltpu.get_barrier_semaphore()

    def greet(i, carry):
        side, other = any_peer(i)
        device = (side * 8 + dp % 8, other)
        pl.semaphore_signal(barrier, inc=1, device_id=device, device_id_type=MESH)
        return carry

    def greet_plane(j, carry):
        pl.semaphore_signal(
            barrier, inc=1, device_id={"dp": plane_peer(j)[1]}, device_id_type=MESH
        )
        return carry

    lax.fori_loop(0, 2 * CTX - 1, greet, 0)
    lax.fori_loop(0, 7, greet_plane, 0)

    def selection(shape, where):
        row = lax.broadcasted_iota(jnp.int32, shape, 0)
        col = lax.broadcasted_iota(jnp.int32, shape, 1)
        return jnp.where(where(row, col), 1.0, 0.0).astype(BF16)

    perm[...] = selection((256, 256), lambda i, j: j == (i % 16) * 16 + i // 16)

    def column(line, count):
        r = lax.broadcasted_iota(jnp.int32, (count, count), 0)
        c = lax.broadcasted_iota(jnp.int32, (count, count), 1)
        return jnp.sum(jnp.where(r == c, line, 0.0), axis=1, keepdims=True)

    def multiply(left, right, target, send):
        for g in range(2):

            def block(r, carry, g=g):
                lanes = pl.ds(pl.multiple_of(r * N, N), N)
                a = left[g * 16 : g * 16 + 16, lanes].astype(F32)
                b = right[g * 16 : g * 16 + 16, lanes].astype(F32)
                target[g, pl.ds(pl.multiple_of(r * 16, 16), 16), :] = (a * b).astype(BF16)
                return carry

            lax.fori_loop(0, ROWS, block, 0, unroll=4)
            send[g] = dot(perm[...], target[g]).astype(BF16).reshape(16, 16, N)

    def exchange(k, send, recv):
        def copy(i):
            return pltpu.make_async_remote_copy(
                src_ref=send.at[:, ctx_peer(i)],
                dst_ref=recv.at[:, me],
                send_sem=ctx_send.at[k, i],
                recv_sem=ctx_recv.at[k, i],
                device_id={"ctx": ctx_peer(i)},
                device_id_type=MESH,
            )

        return copy

    def among(k, send, recv):
        def copy(j):
            return pltpu.make_async_remote_copy(
                src_ref=send(j),
                dst_ref=recv.at[place],
                send_sem=dp_send.at[k, j],
                recv_sem=dp_recv.at[k, j],
                device_id={"dp": plane_peer(j)[1]},
                device_id_type=MESH,
            )

        return copy

    def half_exchange(k, g, send, recv):
        def copy(i):
            return pltpu.make_async_remote_copy(
                src_ref=send.at[g, ctx_peer(i)],
                dst_ref=recv.at[g, me],
                send_sem=ctx_send.at[k, i],
                recv_sem=ctx_recv.at[k, i],
                device_id={"ctx": ctx_peer(i)},
                device_id_type=MESH,
            )

        return copy

    def small_exchange(k, send, recv):
        def copy(i):
            return pltpu.make_async_remote_copy(
                src_ref=send.at[ctx_peer(i)],
                dst_ref=recv.at[me],
                send_sem=ctx_send.at[k, i],
                recv_sem=ctx_recv.at[k, i],
                device_id={"ctx": ctx_peer(i)},
                device_id_type=MESH,
            )

        return copy

    def over(copy, action, count=CTX - 1, begin=0):
        def one(i, carry):
            getattr(copy(i), action)()
            return carry

        lax.fori_loop(begin, count, one, 0)

    def keep(send, recv):
        recv[:, pl.ds(me, 1)] = send[:, pl.ds(me, 1)]

    swap = selection((128, 128), lambda i, j: j == (i % 8) * 16 + i // 8)
    loads[2].wait()
    loads[3].wait()
    decay_column = column(decay[...], 16)

    def envelope(start, width):
        place = start + lax.broadcasted_iota(jnp.int32, (16, width), 1)
        place = (me * LOCAL + place).astype(F32)
        return jnp.exp(-decay_column * (place * (1.0 / SEQ)))

    def taps_row(r, carry):
        start = pl.multiple_of((core * 8 + r) * N + my_y * QUARTER, QUARTER)
        raw = fr[:, pl.ds(start, QUARTER)].astype(F32)
        made = (raw * envelope(start, QUARTER) * SCALE).astype(BF16)
        turned[pl.ds(pl.multiple_of(r * 16, 16), 16), 0:QUARTER] = made
        return carry

    lax.fori_loop(0, 8, taps_row, 0)
    arranged = dot(swap, turned[0:128, 0:QUARTER])
    send_t[...] = arranged.reshape(16, 8, QUARTER).astype(BF16)
    pl.semaphore_wait(barrier, 2 * CTX - 1 + 7)
    copy_t = small_exchange(0, send_t, taps_q.at[place])
    over(copy_t, "start")
    loads[0].wait()
    loads[1].wait()
    multiply(ig, va, mixed, send_m)
    copy_m = exchange(1, send_m, recv_m)
    over(copy_m, "start")
    loads[4].wait()
    loads[5].wait()
    multiply(ct, og, weighted, send_w)
    copy_w = exchange(2, send_w, recv_w)
    over(copy_w, "start")
    taps_q[pl.ds(place, 1), pl.ds(me, 1)] = send_t[pl.ds(me, 1)][None]
    keep(send_m, recv_m)
    keep(send_w, recv_w)

    loads[6].wait()
    loads[7].wait()
    loads[8].wait()
    cosine, sine = roots[0], roots[1]
    first[0:N, 0:HALF] = cosine[:, 0:HALF]
    first[0:N, HALF:N] = sine[:, 0:HALF]
    first[N:, 0:HALF] = -sine[:, 0:HALF]
    first[N:, HALF:N] = cosine[:, 0:HALF]
    first_back[0:HALF, 0:N] = cosine[0:HALF]
    first_back[0:HALF, N:] = -sine[0:HALF]
    first_back[HALF:, 0:N] = sine[0:HALF]
    first_back[HALF:, N:] = cosine[0:HALF]
    gather = selection(
        (256, 256), lambda i, j: j == ((i % 128) // 8) * 16 + (i // 128) * 8 + i % 8
    )
    scatter = selection(
        (256, 256), lambda i, j: i == ((j % 128) // 8) * 16 + (j // 128) * 8 + j % 8
    )
    first_taps[...] = dot(first[:, 0:HALF], scatter).astype(BF16)
    first_lag[...] = dot(gather, first_back[0:HALF, :]).astype(BF16)
    second[0:N, 0:N] = cosine
    second[0:N, N:] = -sine
    second[N:, 0:N] = sine
    second[N:, N:] = cosine
    second_back[0:N, 0:N] = cosine
    second_back[0:N, N:] = sine
    second_back[N:, 0:N] = -sine
    second_back[N:, N:] = cosine
    fine_r, fine_i = turns[0, 32:48, :], turns[1, 32:48, :]

    def turn_rows(a, carry):
        rows = pl.ds(pl.multiple_of(a * 16, 16), 16)
        tr, ti = times(turns[0, pl.ds(a, 1), :], turns[1, pl.ds(a, 1), :], fine_r, fine_i)
        wr[rows, :] = tr
        wi[rows, :] = ti
        return carry

    lax.fori_loop(0, N // 16, turn_rows, 0)

    over(copy_t, "wait_recv")

    share_t = among(0, lambda j: taps_q.at[place], taps_q)
    over(share_t, "start", 7)
    over(share_t, "wait_recv", 7)
    for p in range(8):
        y, half = p // 2, p % 2
        piece = taps_q[p].astype(F32).reshape(128, QUARTER).astype(BF16)
        taps[half * 128 : (half + 1) * 128, y * QUARTER : (y + 1) * QUARTER] = piece

    def forward(start, table, block):
        rows = pl.ds(start, CHUNK)
        pr = dot(table[rows, :], block)
        pi = dot(table[pl.ds(start + N, CHUNK), :], block)
        return dot(joined(*times(pr, pi, wr[rows, :], wi[rows, :])), second[...])

    def backward(start, spectrum, target):
        rows = pl.ds(start, CHUNK)
        br, bi = parts(dot(spectrum, second_back[...]))
        sr, si = conj_times(wr[rows, :], wi[rows, :], br, bi)
        target[rows, :] = (sr * (1.0 / FFT_LEN)).astype(BF16)
        target[pl.ds(start + N, CHUNK), :] = (si * (1.0 / FFT_LEN)).astype(BF16)

    def chunks(body):
        def one(i, carry):
            body(pl.multiple_of(i * CHUNK, CHUNK))
            return carry

        lax.fori_loop(0, N // CHUNK, one, 0)

    def filter_chunk(start):
        spec_h[pl.ds(start, CHUNK), :] = forward(start, first_taps, taps[...]).astype(BF16)

    chunks(filter_chunk)

    over(copy_m, "wait_recv")

    def mix_chunk(start):
        rows = pl.ds(start, CHUNK)
        spectrum = forward(start, first, recv_m[...].reshape(N, N))
        spec_m[rows, :] = spectrum
        hr, hi = parts(spec_h[rows, :].astype(F32))
        backward(start, joined(*times(*parts(spectrum), hr, hi)), turned)

    chunks(mix_chunk)
    for g in range(2):
        made = dot(first_back[g * HALF : (g + 1) * HALF, :], turned[...])
        send_c[g] = made.astype(BF16).reshape(16, 16, N)
    copy_c = exchange(3, send_c, recv_c)
    over(copy_c, "start")
    keep(send_c, recv_c)

    over(copy_w, "wait_recv")

    def weight_chunk(start):
        rows = pl.ds(start, CHUNK)
        spectrum = forward(start, first, recv_w[...].reshape(N, N))
        spec_w[rows, :] = spectrum
        mr, mi = parts(spec_m[rows, :])
        backward(start, joined(*conj_times(mr, mi, *parts(spectrum))), turned_lag)

    chunks(weight_chunk)
    lagged = dot(first_lag[...], turned_lag[...]).astype(BF16)
    for p in range(8):
        y, half = p // 2, p % 2
        lag_q[p] = lagged[half * 128 : (half + 1) * 128, y * QUARTER : (y + 1) * QUARTER]

    copy_s = among(1, lambda j: lag_q.at[plane_peer(j)[0]], lag_y)
    over(copy_s, "start", 7)
    lag_y[pl.ds(place, 1)] = lag_q[pl.ds(place, 1)]

    def correlate_chunk(start):
        rows = pl.ds(start, CHUNK)
        hr, hi = parts(spec_h[rows, :].astype(F32))
        backward(start, joined(*conj_times(hr, hi, *parts(spec_w[rows, :]))), turned)

    chunks(correlate_chunk)
    copy_u = [half_exchange(5 + g, g, send_u, recv_u) for g in range(2)]
    for g in range(2):
        made = dot(first_back[g * HALF : (g + 1) * HALF, :], turned[...])
        send_u[g] = made.astype(BF16).reshape(16, 16, N)
        if g == 0:
            over(copy_u[0], "start", 8)
    over(copy_s, "wait_recv", 7)
    reduced = sum(lag_y[p].astype(F32) for p in range(8))
    lag_z[...] = reduced.reshape(16, 8, QUARTER).astype(BF16)

    def copy_z(i):
        side, other = any_peer(i)
        return pltpu.make_async_remote_copy(
            src_ref=lag_z.at[other],
            dst_ref=lag_f.at[low, me],
            send_sem=lag_send.at[i],
            recv_sem=lag_recv.at[i],
            device_id=(side * 8 + place, other),
            device_id_type=MESH,
        )

    over(copy_z, "start", 2 * CTX - 1)
    over(copy_u[0], "start", begin=8)
    over(copy_u[1], "start")
    lag_f[pl.ds(low, 1), pl.ds(me, 1)] = lag_z[pl.ds(me, 1)][None]
    keep(send_u, recv_u)

    skip_column = column(skip[...], 32)

    def finish(g, recv, base, left, right, first_out, second_out):
        gain = skip_column[g * 16 : g * 16 + 16]
        summed[...] = dot(perm[...], recv[g].reshape(256, N))

        def block(r, carry):
            rows = pl.ds(pl.multiple_of(r * 16, 16), 16)
            lanes = pl.ds(pl.multiple_of(r * N, N), N)
            total = summed[rows, :] + gain * base[g, rows, :].astype(F32)
            place = slice(g * 16, g * 16 + 16)
            first_out[place, lanes] = (left[place, lanes].astype(F32) * total).astype(BF16)
            second_out[place, lanes] = (right[place, lanes].astype(F32) * total).astype(BF16)
            return carry

        lax.fori_loop(0, ROWS, block, 0, unroll=4)

    over(copy_c, "wait_recv")
    for g in range(2):
        finish(g, recv_c, mixed, og, ct, out, gog)
    order = selection(
        (256, 256), lambda i, j: j == (i // 128) * 128 + (i % 16) * 8 + (i % 128) // 16
    )
    over(copy_z, "wait_recv", 2 * CTX - 1)
    both = lag_f[0].astype(F32) + lag_f[1].astype(F32)
    lag_g[pl.ds(place, 1)] = both.reshape(128, QUARTER).astype(BF16)[None]
    copy_g = among(2, lambda j: lag_g.at[place], lag_g)
    over(copy_g, "start", 7)
    over(copy_u[0], "wait_recv")
    finish(0, recv_u, weighted, va, ig, gig, gva)
    over(copy_g, "wait_recv", 7)
    for p in range(8):
        y, half = p // 2, p % 2
        lag[half * 128 : (half + 1) * 128, y * QUARTER : (y + 1) * QUARTER] = lag_g[p]
    summed[...] = dot(order, lag[...])

    def filter_row(r, carry):
        start = pl.multiple_of(r * N, N)
        piece = summed[pl.ds(pl.multiple_of(r * 16, 16), 16), :]
        gf[:, pl.ds(start, N)] = piece * envelope(start, N) * SCALE
        return carry

    lax.fori_loop(0, ROWS, filter_row, 0)
    for copy in (copy_t, copy_m, copy_w, copy_c, *copy_u):
        over(copy, "wait_send")
    for copy in (copy_s, copy_g, share_t):
        over(copy, "wait_send", 7)
    over(copy_z, "wait_send", 2 * CTX - 1)
    over(copy_u[1], "wait_recv")
    finish(1, recv_u, weighted, va, ig, gig, gva)


def store_kernel(*refs):
    copies = [
        pltpu.make_async_copy(source, target, refs[10].at[i])
        for i, (source, target) in enumerate(zip(refs[:5], refs[5:10]))
    ]
    for copy in copies:
        copy.start()
    for copy in copies:
        copy.wait()


def shards(input_gate, output_gate, values, cotangent, filter_raw, filter_decay, skip_gain):
    roots, turns = constant_tables()
    signal = pltpu.VMEM((32, LOCAL), BF16)
    blocks = pltpu.VMEM((2, CTX, ROWS, N), BF16)
    pieces = pltpu.VMEM((8, 128, QUARTER), BF16)
    kept = pltpu.VMEM((16, LOCAL), F32)
    inside = pl.BlockSpec(memory_space=pltpu.VMEM)
    anywhere = pl.BlockSpec(memory_space=pl.ANY)
    made = pl.pallas_call(
        kernel,
        out_shape=(signal, signal, signal, signal, kept),
        in_specs=[pl.BlockSpec(memory_space=pltpu.HBM)] * 9,
        out_specs=(inside,) * 5,
        scratch_shapes=[
            signal, signal, signal, signal,
            pltpu.VMEM((16, LOCAL), BF16),
            pltpu.VMEM((1, 16), F32),
            pltpu.VMEM((1, 32), F32),
            pltpu.VMEM((2, N, N), BF16),
            pltpu.VMEM((2, 48, N), F32),
            pltpu.VMEM((2 * N, N), BF16),
            pltpu.VMEM((N, 2 * N), BF16),
            pltpu.VMEM((HALF, 2 * N), BF16),
            pltpu.VMEM((2 * N, HALF), BF16),
            pltpu.VMEM((2 * N, 2 * N), BF16),
            pltpu.VMEM((2 * N, 2 * N), BF16),
            pltpu.VMEM((N, N), F32),
            pltpu.VMEM((N, N), F32),
            pltpu.VMEM((256, 256), BF16),
            pltpu.VMEM((2, 256, N), BF16),
            pltpu.VMEM((2, 256, N), BF16),
            blocks, blocks, blocks, blocks,
            pltpu.VMEM((CTX, 8, QUARTER), BF16),
            pltpu.VMEM((8, CTX, 8, QUARTER), BF16),
            pltpu.VMEM((256, N), BF16),
            pltpu.VMEM((N, 2 * N), BF16),
            pltpu.VMEM((N, 2 * N), F32),
            pltpu.VMEM((N, 2 * N), F32),
            pltpu.VMEM((2 * N, N), BF16),
            pltpu.VMEM((2 * N, N), BF16),
            blocks, blocks, blocks, blocks,
            pltpu.VMEM((256, N), F32),
            pieces,
            pieces,
            pltpu.VMEM((CTX, 8, QUARTER), BF16),
            pltpu.VMEM((2, CTX, 8, QUARTER), BF16),
            pieces,
            pltpu.VMEM((256, N), BF16),
            pltpu.SemaphoreType.DMA((9,)),
            pltpu.SemaphoreType.DMA((7, CTX - 1)),
            pltpu.SemaphoreType.DMA((7, CTX - 1)),
            pltpu.SemaphoreType.DMA((3, 7)),
            pltpu.SemaphoreType.DMA((3, 7)),
            pltpu.SemaphoreType.DMA((2 * CTX - 1,)),
            pltpu.SemaphoreType.DMA((2 * CTX - 1,)),
        ],
        compiler_params=pltpu.CompilerParams(
            collective_id=0, has_side_effects=True, vmem_limit_bytes=48 << 20
        ),
    )(
        *[
            pltpu.with_memory_space_constraint(x, pltpu.HBM)
            for x in (
                input_gate, values, cotangent, output_gate, filter_raw,
                filter_decay.reshape(1, 16), skip_gain.reshape(1, 32), jnp.asarray(roots), jnp.asarray(turns),
            )
        ]
    )
    big = jax.ShapeDtypeStruct((32, LOCAL), BF16)
    return pl.pallas_call(
        store_kernel,
        out_shape=(big, big, big, big, jax.ShapeDtypeStruct((16, LOCAL), F32)),
        in_specs=[inside] * 5,
        out_specs=(anywhere,) * 5,
        scratch_shapes=[pltpu.SemaphoreType.DMA((5,))],
        compiler_params=pltpu.CompilerParams(vmem_limit_bytes=8 << 20),
    )(*made)


def solution(mesh):
    return jax.shard_map(
        shards,
        mesh=mesh,
        in_specs=(
            P("dp", "ctx"),
            P("dp", "ctx"),
            P("dp", "ctx"),
            P("dp", "ctx"),
            P(None, "ctx"),
            P(),
            P("dp"),
        ),
        out_specs=(P("dp", "ctx"), P("dp", "ctx"), P("dp", "ctx"), P("dp", "ctx"), P(None, "ctx")),
        check_vma=False,
    )
```
